32 devices in a mesh: shard: 2 (over y), ctx: 8 (over z, x), tp: 2 (over core).
Axes of the slice: x: 2, y: 2, z: 4, core: 2. Of those that a mesh axis runs over, the one named last changes fastest.
Arguments:
- tokens: bfloat16 [8192, 768], P(('shard', 'ctx')), may hold values from -6 to 6
- teacher: bfloat16 [8192, 768], P(('shard', 'ctx')), may hold values from -6 to 6
- w_qkv: bfloat16 [768, 3, 768], P('shard', None, 'tp'), may hold values from -0.21875 to 0.21875
- b_qv: float32 [2, 768], P(None, 'tp'), may hold values from -3 to 3
- w_out: bfloat16 [768, 768], P('shard', 'tp'), may hold values from -6 to 6
- w_up: bfloat16 [768, 3072], P('shard', 'tp'), may hold values from -0.21875 to 0.21875
- b_up: float32 [3072], P('tp'), may hold values from -3 to 3
- w_down: bfloat16 [768, 3072], P('shard', 'tp'), may hold values from -0.15625 to 0.15625
- biases: float32 [4, 768], replicated, may hold values from -2 to 2
- gains: float32 [2, 768], replicated, may hold values from 0.25 to 1.75
- lengths: int32 [2], P('shard'), may hold values from 2048 to 4096
- prefix: int32 [2], P('shard'), may hold values from 409 to 2048
- pairing: int32 [2, 12], P('shard', 'tp'), may hold values from 0 to 1
Outputs:
- output: float32 [8192, 768], P(('shard', 'ctx'))
- loss: float32 [], replicated
- grad_tokens: float32 [8192, 768], P(('shard', 'ctx'))
- grad_w_qkv: float32 [768, 3, 768], P('shard', None, 'tp')
- grad_w_out: float32 [768, 768], P('shard', 'tp')
- grad_w_up: float32 [768, 3072], P('shard', 'tp')
- grad_w_down: float32 [768, 3072], P('shard', 'tp')
- grad_b_qv: float32 [2, 768], P(None, ('tp', 'shard'))
- grad_b_up: float32 [3072], P(('tp', 'shard'))
- grad_biases: float32 [4, 768], P(None, 'shard')
- grad_gains: float32 [2, 768], P(None, 'shard')
The draws below stay inside these ranges and needn't reach their ends.
All inputs are finite; a program needn't handle non-finite values.
Results may differ from the reference program's by a relative error of at most 0.014.
Values may be sent and summed in bfloat16 or wider, within the bound.
No kernel may reach another device: no remote copies, remote signals or barrier semaphores. Data moves between devices by JAX's collectives and lax.ppermute only.
A program may use at most 128 MiB of HBM per device.

```python
import jax
import jax.numpy as jnp
from jax import lax

D = 768
H = 12
DH = 64
FF = 3072
LEN = 4096
SEQS = 2
TOKENS = 8192


def touch_ends(drawn, rng, least, high):
    place = [jax.random.randint(jax.random.fold_in(rng, axis), (), 0, length) for axis, length in enumerate(drawn.shape)]
    widest = drawn.shape.index(max(drawn.shape))
    beside = place[:widest] + [(place[widest] + 1) % drawn.shape[widest]] + place[widest + 1:]
    return drawn.at[tuple(place)].set(least).at[tuple(beside)].set(high)


def steps_of(own_key, dims, split, low, largest):
    loudness = 1.0
    for position, blocks in split:
        draws = jax.random.uniform(jax.random.fold_in(jax.random.fold_in(own_key, 6), position), (blocks,), jnp.float32, low / len(split), largest / len(split))
        loudness = loudness * jnp.repeat(jnp.exp(draws), dims[position] // blocks).reshape((-1,) + (1,) * (len(dims) - 1 - position))
    return loudness


def bell_draw(rng, shape, scale, reach, pieces=(), held_as=jnp.bfloat16):
    factor_of = steps_of(rng, shape, pieces, -0.22, 0.18) if pieces else 1.0
    entries = jax.random.normal(rng, shape, jnp.float32) * scale * factor_of
    return jnp.minimum(jnp.maximum(entries, -reach), reach).astype(held_as)


def setup_inputs(seed: int = 0) -> dict:
    key_of = jax.random.split(jax.random.key(seed), 14)
    tokens = bell_draw(key_of[0], (TOKENS, D), 1.0, 6.0, ((0, 16),))
    teacher = bell_draw(key_of[1], (TOKENS, D), 1.0, 6.0, ((0, 16),))
    w_qkv = bell_draw(key_of[2], (D, 3, H * DH), D ** -0.5, 0.21875, ((0, 2), (2, 2)))
    b_qv = bell_draw(key_of[3], (2, H * DH), 0.5, 3.0, ((1, 2),), jnp.float32)
    w_out = bell_draw(key_of[4], (D, H * DH), (max(1, 8 * H * DH // LEN)) ** -0.5, 6.0, ((0, 2), (1, 2)))
    w_up = bell_draw(key_of[5], (D, FF), D ** -0.5, 0.21875, ((0, 2), (1, 2)))
    b_up = bell_draw(key_of[6], (FF,), 0.5, 3.0, ((0, 2),), jnp.float32)
    w_down = bell_draw(key_of[7], (D, FF), (FF // 2) ** -0.5, 0.15625, ((0, 2), (1, 2)))
    biases = bell_draw(key_of[8], (4, D), 0.3, 2.0, (), jnp.float32)
    gains = jnp.clip(1.0 + 0.15 * jax.random.normal(key_of[9], (2, D), jnp.float32), 0.25, 1.75)
    lengths = jax.random.randint(key_of[10], (SEQS,), LEN // 2, LEN + 1).astype(jnp.int32)
    prefix = jax.random.randint(key_of[11], (SEQS,), LEN // 10, LEN // 2 + 1).astype(jnp.int32)
    pairing = touch_ends(jax.random.randint(key_of[12], (SEQS, H), 0, 2), jax.random.fold_in(key_of[12], 1), 0, 1).astype(jnp.int32)
    return dict(tokens=tokens, teacher=teacher, w_qkv=w_qkv, b_qv=b_qv, w_out=w_out, w_up=w_up, b_up=b_up, w_down=w_down, biases=biases, gains=gains, lengths=lengths, prefix=prefix, pairing=pairing)


@jax.custom_vjp
def low(v):
    return lax.optimization_barrier(v.astype(jnp.bfloat16)).astype(jnp.float32)

@jax.custom_vjp
def low_back(v):
    return v

def low_keep(v):
    return (low(v), None)

def low_pass(kept, grad):
    return (grad,)

def back_keep(v):
    return (v, None)

def back_low(kept, grad):
    return (low(grad),)
low.defvjp(low_keep, low_pass)
low_back.defvjp(back_keep, back_low)
HIGH = lax.Precision.HIGHEST

def normalize(rows, gain, shift):
    mean = lax.optimization_barrier(jnp.mean(rows, axis=-1, keepdims=True))
    centered = rows - mean
    spread = lax.optimization_barrier(jnp.mean(centered * centered, axis=-1, keepdims=True))
    return centered * lax.rsqrt(spread + 1e-05) * gain + shift

def gelu_exact(value):
    return 0.5 * value * (1.0 + jax.scipy.special.erf(value * 0.7071067811865476))

def allowed_mask(qpos, kpos, length, first, pairs, seq_len):
    qblock = 2 * qpos // seq_len
    kblock = 2 * kpos // seq_len
    paired = kblock[None, None, :] == qblock[None, :, None] ^ pairs[:, None, None]
    visible = (kpos[None, :] < first) | (kpos[None, :] <= qpos[:, None])
    inside = (qpos[:, None] < length) & (kpos[None, :] < length)
    return paired & (visible & inside)[None]

def attend_rows(qrows, start, keys, values, length, first, pairs):
    rows = qrows.shape[1]
    seq_len = keys.shape[1]
    qpos = start + jnp.arange(rows, dtype=jnp.int32)
    kpos = jnp.arange(seq_len, dtype=jnp.int32)
    allowed = allowed_mask(qpos, kpos, length, first, pairs, seq_len)
    scores = low_back(jnp.einsum('hqd,hkd->hqk', qrows, keys, precision=HIGH) * DH ** (-0.5))
    top = lax.optimization_barrier(jnp.max(jnp.where(allowed, scores, -1e+30), axis=-1, keepdims=True))
    total = lax.optimization_barrier(jnp.sum(jnp.exp(jnp.where(allowed, scores - top, -10000.0)), axis=-1, keepdims=True))
    lse = top + jnp.log(jnp.maximum(total, 1.0))
    probs = low(jnp.exp(jnp.where(allowed, scores - lse, -10000.0)))
    return jnp.einsum('hqk,hkd->hqd', probs, values, precision=HIGH)

def sequence_attention(query, keys, values, length, first, pairs):
    seq_len = query.shape[1]
    size = min(512, seq_len)
    count = seq_len // size
    blocks = query.reshape(H, count, size, DH).transpose(1, 0, 2, 3)
    starts = jnp.arange(count, dtype=jnp.int32) * size

    def one_block(item):
        return attend_rows(item[0], item[1], keys, values, length, first, pairs)
    result = lax.map(jax.checkpoint(one_block), (blocks, starts))
    return result.transpose(1, 0, 2, 3).reshape(H, seq_len, DH)

def forward(xf, wqkv, bqv, wout, wup, bup, wdown, biases, gains, lengths, prefix, pairing):
    query = low(low_back(jnp.dot(xf, wqkv[:, 0, :], precision=HIGH) + bqv[0]))
    keys = low(low_back(jnp.dot(xf, wqkv[:, 1, :], precision=HIGH)))
    values = low(low_back(jnp.dot(xf, wqkv[:, 2, :], precision=HIGH) + bqv[1]))
    seqs = lengths.shape[0]

    def split_heads(t):
        return t.reshape(seqs, -1, H, DH).transpose(0, 2, 1, 3)

    def one_sequence(item):
        return sequence_attention(*item)
    context = lax.map(one_sequence, (split_heads(query), split_heads(keys), split_heads(values), lengths, prefix, pairing))
    context = context.transpose(0, 2, 1, 3).reshape(xf.shape[0], H * DH)
    context = low(low_back(context))
    branch = low_back(jnp.dot(context, wout.T, precision=HIGH) + biases[0])
    hidden = normalize(xf + branch, gains[0], biases[2])
    upper = low_back(jnp.dot(low(hidden), wup, precision=HIGH) + bup)
    active = low(gelu_exact(upper))
    feed = low_back(jnp.dot(active, wdown.T, precision=HIGH) + biases[1])
    return normalize(hidden + feed, gains[1], biases[3])

def reference(tokens, teacher, w_qkv, b_qv, w_out, w_up, b_up, w_down, biases, gains, lengths, prefix, pairing):
    floats = [a.astype(jnp.float32) for a in (tokens, w_qkv, b_qv, w_out, w_up, b_up, w_down, biases, gains)]

    def apply_layer(*params):
        return forward(*params, lengths, prefix, pairing)
    output, pull = jax.vjp(apply_layer, *floats)
    seq_len = tokens.shape[0] // lengths.shape[0]
    positions = jnp.arange(seq_len, dtype=jnp.int32)
    valid = (positions[None, :] < lengths[:, None]).reshape(-1, 1)
    error = jnp.where(valid, output - teacher.astype(jnp.float32), 0.0)
    grads = pull(error)
    count = jnp.sum(valid.astype(jnp.float32))
    loss = jnp.sum(error * error) / (count * D)
    return (output, loss, grads[0], grads[1], grads[3], grads[4], grads[6], grads[2], grads[5], grads[7], grads[8])
```

```python
import functools

import jax
import jax.numpy as jnp
from jax import lax
from jax.experimental import pallas as pl
from jax.experimental.pallas import tpu as pltpu
from jax.sharding import PartitionSpec as P

DH = 64
F32 = jnp.float32
BF16 = jnp.bfloat16
LOW = -1e30


def normalize(rows, gain, shift):
    mean = jnp.mean(rows, axis=-1, keepdims=True)
    centered = rows - mean
    spread = jnp.mean(centered * centered, axis=-1, keepdims=True)
    return centered * lax.rsqrt(spread + 1e-05) * gain + shift


def gelu_exact(value):
    return 0.5 * value * (1.0 + jax.scipy.special.erf(value * 0.7071067811865476))


def flip(x, axis, d):
    n = lax.axis_size(axis)
    return lax.ppermute(x, axis, [(i, i ^ d) for i in range(n)])


def tp_sum(part):
    return part.astype(F32) + flip(part, "tp", 1).astype(F32)


def gather_rows(x):
    if lax.axis_size("shard") != 2:
        return lax.all_gather(x, "shard", axis=0, tiled=True)
    other = flip(x, "shard", 1)
    first = lax.axis_index("shard") == 0
    return jnp.concatenate([jnp.where(first, x, other), jnp.where(first, other, x)], axis=0)


def gather_ctx_halves(x):
    n = lax.axis_size("ctx")
    rows = x.shape[0] // 2
    t = lax.axis_index("tp")
    mine = lax.dynamic_slice_in_dim(x, t * rows, rows, 0)
    if n == 8:
        c = {}
        for d in (4, 2, 6, 1):
            c[d] = flip(mine, "ctx", d)
        for d in (2, 4, 6):
            c[d + 1] = flip(c[d], "ctx", 1)
    else:
        at = lax.axis_index("ctx")
        every = lax.all_gather(mine, "ctx", axis=0, tiled=False)
        c = {d: lax.dynamic_index_in_dim(every, at ^ d, 0, False) for d in range(1, n)}
    return {d: (c[d], flip(c[d], "tp", 1)) for d in c}


def gather_ctx(x):
    n = lax.axis_size("ctx")
    if n == 8:
        return jnp.stack([x] + [flip(x, "ctx", d) for d in range(1, n)])
    at = lax.axis_index("ctx")
    every = lax.all_gather(x, "ctx", axis=0, tiled=False)
    return jnp.stack([lax.dynamic_index_in_dim(every, at ^ d, 0, False) for d in range(n)])


def shard_scatter(x):
    n = lax.axis_size("shard")
    if n != 2:
        return lax.psum_scatter(x, "shard", scatter_dimension=0, tiled=True)
    s = lax.axis_index("shard")
    rows = x.shape[0] // 2
    keep = lax.dynamic_slice_in_dim(x, s * rows, rows, 0)
    send = lax.dynamic_slice_in_dim(x, (1 - s) * rows, rows, 0)
    return keep.astype(F32) + flip(send, "shard", 1).astype(F32)


def ctx_sum(x):
    n = lax.axis_size("ctx")
    d = 1
    while d < n:
        x = x + flip(x, "ctx", d)
        d *= 2
    return x


def params(limit=48 << 20):
    return pltpu.CompilerParams(vmem_limit_bytes=limit)


def dot_nn(a, b):
    return lax.dot_general(a, b, (((1,), (0,)), ((), ())), preferred_element_type=F32)


def dot_nt(a, b):
    return lax.dot_general(a, b, (((1,), (1,)), ((), ())), preferred_element_type=F32)


def project_kernel(info, mine, other, w, bias, *rest):
    out = rest[-1]
    rows = mine.shape[0]
    t = info[0]
    start = pl.multiple_of(t * rows, rows)
    away = pl.multiple_of((1 - t) * rows, rows)
    out[0, pl.ds(start, rows), :] = (dot_nn(mine[...], w[...]) + bias[...]).astype(BF16)
    out[0, pl.ds(away, rows), :] = (dot_nn(other[...], w[...]) + bias[...]).astype(BF16)


def project_into(buffer, n, d, t, mine, other, w, bias):
    rows, width = mine.shape
    cols = w.shape[1]
    whole = lambda shape: pl.BlockSpec(shape, lambda i, info: (0,) * len(shape))
    in_specs = [whole((rows, width)), whole((rows, width)), whole((width, cols)), whole((1, cols))]
    args = [mine, other, w, bias]
    aliases = {}
    if buffer is not None:
        in_specs.append(pl.BlockSpec(memory_space=pl.ANY))
        args.append(buffer)
        aliases = {5: 0}
    return pl.pallas_call(
        project_kernel,
        grid_spec=pltpu.PrefetchScalarGridSpec(
            num_scalar_prefetch=1,
            grid=(1,),
            in_specs=in_specs,
            out_specs=pl.BlockSpec((1, 2 * rows, cols), lambda i, info: (d, 0, 0)),
        ),
        out_shape=jax.ShapeDtypeStruct((n, 2 * rows, cols), BF16),
        input_output_aliases=aliases,
        compiler_params=params(),
        name="project",
    )(t, *args)


def lane_groups(op, value):
    out = value[:, :128]
    for g in range(1, value.shape[1] // 128):
        out = op(out, value[:, g * 128 : (g + 1) * 128])
    return out


def allowed_of(qpos, kpos, first, length):
    return ((kpos < first) | (kpos <= qpos)) & (kpos < length)


def attend_kernel(n, info, q_ref, k_ref, v_ref, o_ref, or_ref, lse_ref, lrow_ref, s_scr, mx, tot, acc):
    p = pl.program_id(0)
    c, length, first = info[0], info[1], info[2]
    half = n // 2
    tok = q_ref.shape[1]
    my_block = c // half
    lane = lax.broadcasted_iota(jnp.int32, (1, 128), 1)
    row = lax.broadcasted_iota(jnp.int32, (tok, 1), 0) + c * tok
    q2 = q_ref[0] * jnp.asarray(DH**-0.5, BF16)
    outs = []

    @pl.when(p == 0)
    def _():
        lse_ref[...] = jnp.zeros_like(lse_ref)

    for j in range(2):
        pair = info[3 + 2 * p + j]
        in_head = (lane < 64) if j == 0 else (lane >= 64)
        qm = jnp.where(in_head, q2, jnp.zeros_like(q2))
        some = jnp.logical_not((pair == 1) & (my_block == 0))
        block = my_block ^ pair
        mx[...] = jnp.full_like(mx, LOW)
        tot[...] = jnp.zeros_like(tot)
        acc[...] = jnp.zeros_like(acc)

        def where_is(i):
            kstart = (block * half + ((c % half) ^ i)) * tok
            reach = jnp.where(pair == 1, n * tok, jnp.maximum(first, (c + 1) * tok))
            needed = some & (kstart < jnp.minimum(length, reach))
            clear = jnp.where(pair == 1, n * tok, jnp.maximum(first, c * tok + 1))
            full = kstart + tok <= jnp.minimum(length, clear)
            return kstart, needed, full

        def scores(i, _):
            kstart, needed, full = where_is(i)

            @pl.when(needed)
            def _():
                s = dot_nt(qm, k_ref[i + pair * half])
                s_scr[i] = s

                @pl.when(full)
                def _():
                    mx[...] = jnp.maximum(mx[...], lane_groups(jnp.maximum, s))

                @pl.when(jnp.logical_not(full))
                def _():
                    kpos = kstart + lax.broadcasted_iota(jnp.int32, (1, tok), 1)
                    sm = jnp.where(allowed_of(row, kpos, first, length), s, LOW)
                    s_scr[i] = sm
                    mx[...] = jnp.maximum(mx[...], lane_groups(jnp.maximum, sm))

            return 0

        lax.fori_loop(0, half, scores, 0)
        m = jnp.max(mx[...], axis=1, keepdims=True)

        def values(i, _):
            _, needed, _ = where_is(i)

            @pl.when(needed)
            def _():
                e = jnp.exp(s_scr[i] - m)
                tot[...] += lane_groups(jnp.add, e)
                acc[...] += dot_nn(e.astype(BF16), v_ref[i + pair * half])

            return 0

        lax.fori_loop(0, half, values, 0)
        total = jnp.maximum(jnp.sum(tot[...], axis=1, keepdims=True), 1.0)
        good = some & (row < length)
        lse = jnp.where(good, m + jnp.log(total), LOW)
        lse_ref[...] = jnp.where(lane == 2 * p + j, lse, lse_ref[...])
        outs.append(jnp.where(good, acc[...] / total, 0.0))
    o = jnp.where(lane < 64, outs[0], outs[1])
    o_ref[...] = o
    or_ref[...] = o.astype(BF16)

    @pl.when(p == pl.num_programs(0) - 1)
    def _():
        lrow_ref[...] = lse_ref[...].T[:8]


def attend(info, qkv, heads):
    n, tok, _ = qkv.shape
    pairs = heads // 2
    col = lambda at: pl.BlockSpec((n, tok, 128), lambda p, info: (0, 0, at + p))
    return pl.pallas_call(
        functools.partial(attend_kernel, n),
        grid_spec=pltpu.PrefetchScalarGridSpec(
            num_scalar_prefetch=1,
            grid=(pairs,),
            in_specs=[
                pl.BlockSpec((1, tok, 128), lambda p, info: (0, 0, p)),
                col(pairs),
                col(2 * pairs),
            ],
            out_specs=[
                pl.BlockSpec((tok, 128), lambda p, info: (0, p)),
                pl.BlockSpec((tok, 128), lambda p, info: (0, p)),
                pl.BlockSpec((tok, 128), lambda p, info: (0, 0)),
                pl.BlockSpec((8, tok), lambda p, info: (0, 0)),
            ],
            scratch_shapes=[
                pltpu.VMEM((n // 2, tok, tok), F32),
                pltpu.VMEM((tok, 128), F32),
                pltpu.VMEM((tok, 128), F32),
                pltpu.VMEM((tok, 128), F32),
            ],
        ),
        out_shape=[
            jax.ShapeDtypeStruct((tok, heads * DH), F32),
            jax.ShapeDtypeStruct((tok, heads * DH), BF16),
            jax.ShapeDtypeStruct((tok, 128), F32),
            jax.ShapeDtypeStruct((8, tok), F32),
        ],
        compiler_params=params(),
        name="attend",
    )(info, qkv, qkv, qkv)


def context_grad_kernel(gb, w, o, do_ref, delta_ref, drow_ref):
    do = dot_nn(gb[...], w[...]).astype(BF16)
    do_ref[...] = do
    prod = do.astype(F32) * o[...]
    lane = lax.broadcasted_iota(jnp.int32, (1, 128), 1)
    delta = jnp.zeros(delta_ref.shape, F32)
    for g in range(prod.shape[1] // 128):
        piece = prod[:, g * 128 : (g + 1) * 128]
        for j in range(2):
            in_head = (lane < 64) if j == 0 else (lane >= 64)
            value = jnp.sum(jnp.where(in_head, piece, 0.0), axis=1, keepdims=True)
            delta = jnp.where(lane == 2 * g + j, value, delta)
    delta_ref[...] = delta
    drow_ref[...] = delta.T[:8]


def context_grad(gb, w, o):
    tok, cols = o.shape
    return pl.pallas_call(
        context_grad_kernel,
        out_shape=[
            jax.ShapeDtypeStruct((tok, cols), BF16),
            jax.ShapeDtypeStruct((tok, 128), F32),
            jax.ShapeDtypeStruct((8, tok), F32),
        ],
        compiler_params=params(),
        name="context_grad",
    )(gb, w, o)


def query_grad_kernel(n, info, q_ref, k_ref, v_ref, do_ref, lse_ref, delta_ref, dq_ref, acc):
    p = pl.program_id(0)
    c, length, first = info[0], info[1], info[2]
    half = n // 2
    tok = q_ref.shape[1]
    my_block = c // half
    lane = lax.broadcasted_iota(jnp.int32, (1, 128), 1)
    row = lax.broadcasted_iota(jnp.int32, (tok, 1), 0) + c * tok
    q2 = q_ref[0] * jnp.asarray(DH**-0.5, BF16)
    do2 = do_ref[...]
    outs = []
    for j in range(2):
        pair = info[3 + 2 * p + j]
        in_head = (lane < 64) if j == 0 else (lane >= 64)
        qm = jnp.where(in_head, q2, jnp.zeros_like(q2))
        dom = jnp.where(in_head, do2, jnp.zeros_like(do2))
        some = jnp.logical_not((pair == 1) & (my_block == 0))
        block = my_block ^ pair
        pick = lane == 2 * p + j
        lse = jnp.sum(jnp.where(pick, lse_ref[...], 0.0), axis=1, keepdims=True)
        lse = jnp.where(row < length, lse, -LOW)
        delta = jnp.sum(jnp.where(pick, delta_ref[...], 0.0), axis=1, keepdims=True)
        acc[...] = jnp.zeros_like(acc)

        def chunk(i, _):
            kstart = (block * half + ((c % half) ^ i)) * tok
            reach = jnp.where(pair == 1, n * tok, jnp.maximum(first, (c + 1) * tok))
            needed = some & (kstart < jnp.minimum(length, reach))
            clear = jnp.where(pair == 1, n * tok, jnp.maximum(first, c * tok + 1))
            full = kstart + tok <= jnp.minimum(length, clear)

            def work(masked):
                k = k_ref[i + pair * half]
                s = dot_nt(qm, k)
                if masked:
                    kpos = kstart + lax.broadcasted_iota(jnp.int32, (1, tok), 1)
                    s = jnp.where(allowed_of(row, kpos, first, length), s, LOW)
                e = jnp.exp(s - lse)
                dp = dot_nt(dom, v_ref[i + pair * half])
                ds = (e * (dp - delta)).astype(BF16)
                acc[...] += dot_nn(ds, k)

            @pl.when(needed & full)
            def _():
                work(False)

            @pl.when(needed & jnp.logical_not(full))
            def _():
                work(True)

            return 0

        lax.fori_loop(0, half, chunk, 0)
        outs.append(acc[...])
    dq_ref[...] = (jnp.where(lane < 64, outs[0], outs[1]) * DH**-0.5).astype(BF16)


def query_grad(info, qkv, do, lse, delta, heads):
    n, tok, _ = qkv.shape
    pairs = heads // 2
    col = lambda at: pl.BlockSpec((n, tok, 128), lambda p, info: (0, 0, at + p))
    own = pl.BlockSpec((tok, 128), lambda p, info: (0, p))
    stat = pl.BlockSpec((tok, 128), lambda p, info: (0, 0))
    return pl.pallas_call(
        functools.partial(query_grad_kernel, n),
        grid_spec=pltpu.PrefetchScalarGridSpec(
            num_scalar_prefetch=1,
            grid=(pairs,),
            in_specs=[
                pl.BlockSpec((1, tok, 128), lambda p, info: (0, 0, p)),
                col(pairs),
                col(2 * pairs),
                own,
                stat,
                stat,
            ],
            out_specs=own,
            scratch_shapes=[pltpu.VMEM((tok, 128), F32)],
        ),
        out_shape=jax.ShapeDtypeStruct((tok, heads * DH), BF16),
        compiler_params=params(),
        name="query_grad",
    )(info, qkv, qkv, qkv, do, lse, delta)


def key_grad_kernel(n, info, q_ref, k_ref, v_ref, do_ref, lse_ref, delta_ref, dk_ref, dv_ref, kacc, vacc):
    p = pl.program_id(0)
    c, length, first = info[0], info[1], info[2]
    half = n // 2
    tok = k_ref.shape[1]
    my_block = c // half
    lane = lax.broadcasted_iota(jnp.int32, (1, 128), 1)
    kpos = lax.broadcasted_iota(jnp.int32, (tok, 1), 0) + c * tok
    kstart = c * tok
    k2 = k_ref[0] * jnp.asarray(DH**-0.5, BF16)
    v2 = v_ref[0]
    dks, dvs = [], []
    for j in range(2):
        h = 2 * p + j
        pair = info[3 + h]
        in_head = (lane < 64) if j == 0 else (lane >= 64)
        km = jnp.where(in_head, k2, jnp.zeros_like(k2))
        vm = jnp.where(in_head, v2, jnp.zeros_like(v2))
        some = jnp.logical_not((pair == 1) & (my_block == 1)) & (kstart < length)
        block = my_block ^ pair
        kacc[...] = jnp.zeros_like(kacc)
        vacc[...] = jnp.zeros_like(vacc)

        def chunk(i, _):
            at = block * half + ((c % half) ^ i)
            qstart = at * tok
            d = i + pair * half
            needed = some & (qstart < length) & ((pair == 1) | (at >= c) | (kstart < first))
            full = (pair == 1) | (at > c) | (kstart + tok <= first)

            def work(masked):
                q = q_ref[d]
                do = do_ref[d]
                qpos = qstart + lax.broadcasted_iota(jnp.int32, (1, tok), 1)
                lse = jnp.where(qpos < length, lse_ref[d, pl.ds(h, 1), :], -LOW)
                s = dot_nt(km, q)
                if masked:
                    s = jnp.where((kpos < first) | (kpos <= qpos), s, LOW)
                e = jnp.exp(s - lse)
                vacc[...] += dot_nn(e.astype(BF16), do)
                dp = dot_nt(vm, do)
                ds = (e * (dp - delta_ref[d, pl.ds(h, 1), :])).astype(BF16)
                kacc[...] += dot_nn(ds, q)

            @pl.when(needed & full)
            def _():
                work(False)

            @pl.when(needed & jnp.logical_not(full))
            def _():
                work(True)

            return 0

        lax.fori_loop(0, half, chunk, 0)
        good = kpos < length
        dks.append(jnp.where(good, kacc[...], 0.0))
        dvs.append(jnp.where(good, vacc[...], 0.0))
    dk_ref[...] = (jnp.where(lane < 64, dks[0], dks[1]) * DH**-0.5).astype(BF16)
    dv_ref[...] = jnp.where(lane < 64, dvs[0], dvs[1]).astype(BF16)


def key_grad(info, qkv, do_all, lse_all, delta_all, heads):
    n, tok, _ = qkv.shape
    pairs = heads // 2
    own = lambda at: pl.BlockSpec((1, tok, 128), lambda p, info: (0, 0, at + p))
    every = pl.BlockSpec((n, tok, 128), lambda p, info: (0, 0, p))
    stat = pl.BlockSpec((n, 8, tok), lambda p, info: (0, 0, 0))
    out = pl.BlockSpec((tok, 128), lambda p, info: (0, p))
    return pl.pallas_call(
        functools.partial(key_grad_kernel, n),
        grid_spec=pltpu.PrefetchScalarGridSpec(
            num_scalar_prefetch=1,
            grid=(pairs,),
            in_specs=[every, own(pairs), own(2 * pairs), every, stat, stat],
            out_specs=[out, out],
            scratch_shapes=[pltpu.VMEM((tok, 128), F32), pltpu.VMEM((tok, 128), F32)],
        ),
        out_shape=[jax.ShapeDtypeStruct((tok, heads * DH), BF16)] * 2,
        compiler_params=params(),
        name="key_grad",
    )(info, qkv, qkv, qkv, do_all, lse_all, delta_all)


def place_kernel(n, info, *refs):
    out = refs[-1]
    rows = refs[0].shape[0]
    for d in range(n):
        at = pl.multiple_of((info[0] ^ d) * rows, 8)
        out[pl.ds(at, rows), :] = refs[d][...].astype(F32)


def place(info, parts, limit=1536):
    n = len(parts)
    rows, cols = parts[0].shape
    wide = next(w for w in (384, 128, cols) if cols % w == 0)
    return pl.pallas_call(
        functools.partial(place_kernel, n),
        grid_spec=pltpu.PrefetchScalarGridSpec(
            num_scalar_prefetch=1,
            grid=(cols // wide,),
            in_specs=[pl.BlockSpec((rows, wide), lambda g, info: (0, g))] * n,
            out_specs=pl.BlockSpec((n * rows, wide), lambda g, info: (0, g)),
        ),
        out_shape=jax.ShapeDtypeStruct((n * rows, cols), F32),
        compiler_params=params(),
        name="place",
    )(info, *parts)


def reduce_weight(info, grad):
    n = lax.axis_size("ctx")
    if lax.axis_size("shard") != 2 or n != 8:
        mine = lax.psum_scatter(grad, "shard", scatter_dimension=0, tiled=True)
        return lax.psum(mine, "ctx").astype(F32)
    mine = shard_scatter(grad).astype(BF16)
    rows, cols = mine.shape
    pieces = lax.all_to_all(mine.reshape(n, rows // n, cols), "ctx", 0, 0)
    total = jnp.sum(pieces.astype(F32), axis=0).astype(BF16)
    c = {0: total}
    for d in (4, 2, 6, 1):
        c[d] = flip(total, "ctx", d)
    for d in (2, 4, 6):
        c[d + 1] = flip(c[d], "ctx", 1)
    return place(info, [c[d] for d in range(n)])


def body(
    tokens, teacher, w_qkv, b_qv, w_out, w_up, b_up, w_down, biases, gains, lengths, prefix, pairing
):
    tok, width = tokens.shape
    n_shard = lax.axis_size("shard")
    n = lax.axis_size("ctx")
    c = lax.axis_index("ctx").astype(jnp.int32)
    t = lax.axis_index("tp").astype(jnp.int32)
    length = lengths[0]
    heads = pairing.shape[1]
    hdl = heads * DH
    info = jnp.concatenate([c[None], lengths, prefix, pairing[0]])
    core = t[None]
    zero = jnp.zeros((1,), jnp.int32)

    full_qkv = gather_rows(w_qkv.reshape(w_qkv.shape[0], 3 * hdl))
    token_parts = gather_ctx_halves(tokens)
    full_out = gather_rows(w_out)
    full_up = gather_rows(w_up)
    full_down = gather_rows(w_down)
    ffl = full_up.shape[1]
    bias_qkv = jnp.concatenate([b_qv[0], jnp.zeros((hdl,), F32), b_qv[1]])[None]

    half = tok // 2
    qkv = project_into(None, n, 0, zero, tokens[:half], tokens[half:], full_qkv, bias_qkv)
    for d in sorted(token_parts, key=lambda d: (d % 2, d)):
        qkv = project_into(qkv, n, d, core, *token_parts[d], full_qkv, bias_qkv)
    context, o_r, lse, lse_row = attend(info, qkv, heads)
    lse_all = gather_ctx(lse_row)
    branch = tp_sum(dot_nt(o_r, full_out).astype(BF16)) + biases[0]

    xf = tokens.astype(F32)
    hidden, pull_first = jax.vjp(normalize, xf + branch, gains[0], biases[2])
    hidden_r = hidden.astype(BF16)
    upper = jnp.dot(hidden_r, full_up, preferred_element_type=F32) + b_up
    active, pull_gelu = jax.vjp(gelu_exact, upper)
    active_r = active.astype(BF16)
    feed = tp_sum(dot_nt(active_r, full_down).astype(BF16)) + biases[1]
    output, pull_second = jax.vjp(normalize, hidden + feed, gains[1], biases[3])
    qpos = c * tok + jnp.arange(tok, dtype=jnp.int32)
    valid = (qpos < length)[:, None]
    error = jnp.where(valid, output - teacher.astype(F32), 0.0)
    d_second, d_gain2, d_shift2 = pull_second(error)
    d_feed = d_second.astype(BF16)
    d_active = jnp.dot(d_feed, full_down, preferred_element_type=F32)
    d_upper = pull_gelu(d_active)[0].astype(BF16)
    d_hidden = d_second + tp_sum(dot_nt(d_upper, full_up).astype(BF16))
    d_first, d_gain1, d_shift1 = pull_first(d_hidden)
    d_branch = d_first.astype(BF16)

    branch_parts = gather_ctx_halves(d_branch)
    d_context, delta, delta_row = context_grad(d_branch, full_out, context)
    delta_all = gather_ctx(delta_row)
    dq_r = query_grad(info, qkv, d_context, lse, delta, heads)
    no_bias = jnp.zeros((1, hdl), F32)
    do_all = project_into(None, n, 0, zero, d_branch[:half], d_branch[half:], full_out, no_bias)
    for d in sorted(branch_parts, key=lambda d: (d % 2, d)):
        do_all = project_into(do_all, n, d, core, *branch_parts[d], full_out, no_bias)
    dk_r, dv_r = key_grad(info, qkv, do_all, lse_all, delta_all, heads)
    d_qkv = jnp.concatenate([dq_r, dk_r, dv_r], axis=1)
    grad_tokens = d_first + tp_sum(dot_nt(d_qkv, full_qkv).astype(BF16))

    outer = lambda a, b: lax.dot_general(
        a, b, (((0,), (0,)), ((), ())), preferred_element_type=F32
    ).astype(BF16)
    grad_w_down = reduce_weight(info, outer(d_feed, active_r))
    grad_w_up = reduce_weight(info, outer(hidden_r, d_upper))
    grad_w_out = reduce_weight(info, outer(d_branch, o_r))
    grad_w_qkv = reduce_weight(info, outer(tokens, d_qkv))

    err_sum = jnp.sum(error * error)
    count = jnp.sum(valid.astype(F32))
    split = lambda rows: rows.reshape(rows.shape[0], n_shard, -1).transpose(1, 0, 2).reshape(n_shard, -1)
    early = jnp.concatenate(
        [
            split(jnp.sum(d_branch.astype(F32), axis=0)[None]),
            split(jnp.sum(d_feed.astype(F32), axis=0)[None]),
            split(d_shift1[None]),
            split(d_shift2[None]),
            split(d_gain1[None]),
            split(d_gain2[None]),
            split(jnp.sum(d_upper.astype(F32), axis=0)[None]),
            jnp.full((n_shard, 1), err_sum),
            jnp.full((n_shard, 1), count),
        ],
        axis=1,
    )
    early = ctx_sum(shard_scatter(early))[0]
    late = jnp.concatenate(
        [split(jnp.sum(g.astype(F32), axis=0)[None]) for g in (dq_r, dv_r)], axis=1
    )
    late = ctx_sum(shard_scatter(late))[0]
    wide = width // n_shard
    grad_biases = early[: 4 * wide].reshape(4, wide)
    grad_gains = early[4 * wide : 6 * wide].reshape(2, wide)
    grad_b_up = early[6 * wide : 6 * wide + ffl // n_shard]
    loss = early[-2] / (early[-1] * width)
    grad_b_qv = late.reshape(2, hdl // n_shard)
    return (
        output,
        loss,
        grad_tokens,
        grad_w_qkv.reshape(grad_w_qkv.shape[0], 3, hdl),
        grad_w_out,
        grad_w_up,
        grad_w_down,
        grad_b_qv,
        grad_b_up,
        grad_biases,
        grad_gains,
    )


def solution(mesh):
    return jax.shard_map(
        body,
        mesh=mesh,
        in_specs=(
            P(("shard", "ctx"), None),
            P(("shard", "ctx"), None),
            P("shard", None, "tp"),
            P(None, "tp"),
            P("shard", "tp"),
            P("shard", "tp"),
            P("tp"),
            P("shard", "tp"),
            P(),
            P(),
            P("shard"),
            P("shard"),
            P("shard", "tp"),
        ),
        out_specs=(
            P(("shard", "ctx"), None),
            P(),
            P(("shard", "ctx"), None),
            P("shard", None, "tp"),
            P("shard", "tp"),
            P("shard", "tp"),
            P("shard", "tp"),
            P(None, ("tp", "shard")),
            P(("tp", "shard")),
            P(None, "shard"),
            P(None, "shard"),
        ),
        check_vma=False,
    )
```

```python
import functools

import jax
import jax.numpy as jnp
from jax import lax
from jax.experimental import pallas as pl
from jax.experimental.pallas import tpu as pltpu
from jax.sharding import PartitionSpec as P

DH = 64
F32 = jnp.float32
BF16 = jnp.bfloat16
LOW = -1e30


def normalize(rows, gain, shift):
    mean = jnp.mean(rows, axis=-1, keepdims=True)
    centered = rows - mean
    spread = jnp.mean(centered * centered, axis=-1, keepdims=True)
    return centered * lax.rsqrt(spread + 1e-05) * gain + shift


def gelu_exact(value):
    return 0.5 * value * (1.0 + jax.scipy.special.erf(value * 0.7071067811865476))


def flip(x, axis, d):
    n = lax.axis_size(axis)
    return lax.ppermute(x, axis, [(i, i ^ d) for i in range(n)])


def tp_sum(part):
    return part.astype(F32) + flip(part, "tp", 1).astype(F32)


def join_kernel(at, own, other, out):
    rows = own.shape[1]
    start = pl.multiple_of(at[0] * rows, rows)
    away = pl.multiple_of((1 - at[0]) * rows, rows)
    out[0, pl.ds(start, rows), :] = own[0]
    out[0, pl.ds(away, rows), :] = other[0]


def gather_rows(x):
    if lax.axis_size("shard") != 2:
        return lax.all_gather(x, "shard", axis=1, tiled=True)
    other = flip(x, "shard", 1)
    count, rows, cols = x.shape
    part = pl.BlockSpec((1, rows, cols), lambda i, at: (i, 0, 0))
    return pl.pallas_call(
        join_kernel,
        grid_spec=pltpu.PrefetchScalarGridSpec(
            num_scalar_prefetch=1,
            grid=(count,),
            in_specs=[part, part],
            out_specs=pl.BlockSpec((1, 2 * rows, cols), lambda i, at: (i, 0, 0)),
        ),
        out_shape=jax.ShapeDtypeStruct((count, 2 * rows, cols), x.dtype),
        compiler_params=params(16),
        cost_estimate=cost(1.5),
        name="join",
    )(lax.axis_index("shard").astype(jnp.int32)[None], x, other)


def gather_ctx_halves(x):
    n = lax.axis_size("ctx")
    rows = x.shape[0] // 2
    t = lax.axis_index("tp")
    mine = lax.dynamic_slice_in_dim(x, t * rows, rows, 0)
    if n == 8:
        c = {}
        for d in (4, 2, 6, 1):
            c[d] = flip(mine, "ctx", d)
        for d in (2, 4, 6):
            c[d + 1] = flip(c[d], "ctx", 1)
    else:
        at = lax.axis_index("ctx")
        every = lax.all_gather(mine, "ctx", axis=0, tiled=False)
        c = {d: lax.dynamic_index_in_dim(every, at ^ d, 0, False) for d in range(1, n)}
    return {d: (c[d], flip(c[d], "tp", 1)) for d in c}


def gather_block(x, swapped):
    n = lax.axis_size("ctx")
    half = n // 2
    at = lax.axis_index("ctx")
    low = at < half
    if n == 8:
        away = lax.ppermute(x, "ctx", [(i + half, i) for i in range(half)])
        x = jnp.where(low & swapped, away, x)
        c = {0: x, 2: flip(x, "ctx", 2), 1: flip(x, "ctx", 1)}
        c[3] = flip(c[2], "ctx", 1)
        return [c[i] for i in range(half)]
    every = lax.all_gather(x, "ctx", axis=0, tiled=False)
    pick = lambda d: lax.dynamic_index_in_dim(every, at ^ d, 0, False)
    return [jnp.where(low & swapped, pick(i + half), pick(i)) for i in range(half)]


def after(x, *first):
    return lax.optimization_barrier((x,) + first)[0]


def shard_scatter(x):
    n = lax.axis_size("shard")
    if n != 2:
        return lax.psum_scatter(x, "shard", scatter_dimension=0, tiled=True)
    s = lax.axis_index("shard")
    rows = x.shape[0] // 2
    keep = lax.dynamic_slice_in_dim(x, s * rows, rows, 0)
    send = lax.dynamic_slice_in_dim(x, (1 - s) * rows, rows, 0)
    return keep.astype(F32) + flip(send, "shard", 1).astype(F32)


def ctx_sum(x):
    n = lax.axis_size("ctx")
    d = 1
    while d < n:
        x = x + flip(x, "ctx", d)
        d *= 2
    return x


def params(mib, n=8):
    return pltpu.CompilerParams(vmem_limit_bytes=(mib << 20) * max(1, n // 8))


def cost(us):
    return pl.CostEstimate(flops=int(us * 1e9), bytes_accessed=int(us * 3e6), transcendentals=0)


def dot_nn(a, b):
    return lax.dot_general(a, b, (((1,), (0,)), ((), ())), preferred_element_type=F32)


def dot_nt(a, b):
    return lax.dot_general(a, b, (((1,), (1,)), ((), ())), preferred_element_type=F32)


def project_kernel(count, info, *refs):
    w, bias = refs[2 * count : 2 * count + 2]
    out = refs[-1]
    t = info[0]
    for i in range(count):

        @pl.when(pl.program_id(0) == i)
        def _():
            mine, other = refs[2 * i : 2 * i + 2]
            rows = mine.shape[0]
            start = pl.multiple_of(t * rows, rows)
            away = pl.multiple_of((1 - t) * rows, rows)
            cols = w.shape[2]
            for m in range(w.shape[0]):
                span = slice(m * cols, (m + 1) * cols)
                for at, ref in ((start, mine), (away, other)):
                    value = dot_nn(ref[...], w[m]) + bias[:, span]
                    out[0, pl.ds(at, rows), span] = value.astype(BF16)


def project_into(buffer, n, blocks, t, halves, w, bias):
    rows, width = halves[0][0].shape
    cols = w.shape[0] * w.shape[2]
    count = len(blocks)
    whole = lambda shape: pl.BlockSpec(shape, lambda i, info: (0,) * len(shape))
    in_specs = [whole((rows, width))] * (2 * count) + [whole(w.shape), whole((1, cols))]
    args = [half for pair in halves for half in pair] + [w, bias]
    aliases = {}
    if buffer is not None:
        in_specs.append(pl.BlockSpec(memory_space=pl.ANY))
        aliases = {len(args) + 1: 0}
        args.append(buffer)
    return pl.pallas_call(
        functools.partial(project_kernel, count),
        grid_spec=pltpu.PrefetchScalarGridSpec(
            num_scalar_prefetch=1,
            grid=(count,),
            in_specs=in_specs,
            out_specs=pl.BlockSpec(
                (1, 2 * rows, cols), lambda i, info: (blocks.start + i * blocks.step, 0, 0)
            ),
        ),
        out_shape=jax.ShapeDtypeStruct((n, 2 * rows, cols), BF16),
        input_output_aliases=aliases,
        compiler_params=params(20, n),
        cost_estimate=cost(1 + 1.2 * count),
        name="project",
    )(t, *args)


def lane_groups(op, value):
    out = value[:, :128]
    for g in range(1, value.shape[1] // 128):
        out = op(out, value[:, g * 128 : (g + 1) * 128])
    return out


def allowed_of(qpos, kpos, first, length):
    return ((kpos < first) | (kpos <= qpos)) & (kpos < length)


def attend_kernel(n, info, q_ref, k_ref, v_ref, o_ref, or_ref, lse_ref, lrow_ref, s_scr, mx, tot, acc):
    p = pl.program_id(0)
    c, length, first = info[0], info[1], info[2]
    half = n // 2
    tok = q_ref.shape[1]
    my_block = c // half
    lane = lax.broadcasted_iota(jnp.int32, (1, 128), 1)
    row = lax.broadcasted_iota(jnp.int32, (tok, 1), 0) + c * tok
    q2 = q_ref[0] * jnp.asarray(DH**-0.5, BF16)
    outs = []

    @pl.when(p == 0)
    def _():
        lse_ref[...] = jnp.zeros_like(lse_ref)

    for j in range(2):
        pair = info[3 + 2 * p + j]
        in_head = (lane < 64) if j == 0 else (lane >= 64)
        qm = jnp.where(in_head, q2, jnp.zeros_like(q2))
        some = jnp.logical_not((pair == 1) & (my_block == 0))
        block = my_block ^ pair
        mx[...] = jnp.full_like(mx, LOW)
        tot[...] = jnp.zeros_like(tot)
        acc[...] = jnp.zeros_like(acc)

        def where_is(i):
            kstart = (block * half + ((c % half) ^ i)) * tok
            reach = jnp.where(pair == 1, n * tok, jnp.maximum(first, (c + 1) * tok))
            needed = some & (kstart < jnp.minimum(length, reach))
            clear = jnp.where(pair == 1, n * tok, jnp.maximum(first, c * tok + 1))
            full = kstart + tok <= jnp.minimum(length, clear)
            return kstart, needed, full

        def scores(i, _):
            kstart, needed, full = where_is(i)

            @pl.when(needed)
            def _():
                s = dot_nt(qm, k_ref[i + pair * half])
                s_scr[i] = s

                @pl.when(full)
                def _():
                    mx[...] = jnp.maximum(mx[...], lane_groups(jnp.maximum, s))

                @pl.when(jnp.logical_not(full))
                def _():
                    kpos = kstart + lax.broadcasted_iota(jnp.int32, (1, tok), 1)
                    sm = jnp.where(allowed_of(row, kpos, first, length), s, LOW)
                    s_scr[i] = sm
                    mx[...] = jnp.maximum(mx[...], lane_groups(jnp.maximum, sm))

            return 0

        lax.fori_loop(0, half, scores, 0)
        m = jnp.max(mx[...], axis=1, keepdims=True)

        def values(i, _):
            _, needed, _ = where_is(i)

            @pl.when(needed)
            def _():
                e = jnp.exp(s_scr[i] - m)
                tot[...] += lane_groups(jnp.add, e)
                acc[...] += dot_nn(e.astype(BF16), v_ref[i + pair * half])

            return 0

        lax.fori_loop(0, half, values, 0)
        total = jnp.maximum(jnp.sum(tot[...], axis=1, keepdims=True), 1.0)
        good = some & (row < length)
        lse = jnp.where(good, m + jnp.log(total), LOW)
        lse_ref[...] = jnp.where(lane == 2 * p + j, lse, lse_ref[...])
        outs.append(jnp.where(good, acc[...] / total, 0.0))
    o = jnp.where(lane < 64, outs[0], outs[1])
    o_ref[...] = o
    or_ref[...] = o.astype(BF16)

    @pl.when(p == pl.num_programs(0) - 1)
    def _():
        lrow_ref[...] = lse_ref[...].T[:8]


def attend(info, qkv, heads):
    n, tok, _ = qkv.shape
    pairs = heads // 2
    col = lambda at: pl.BlockSpec((n, tok, 128), lambda p, info: (0, 0, at + p))
    return pl.pallas_call(
        functools.partial(attend_kernel, n),
        grid_spec=pltpu.PrefetchScalarGridSpec(
            num_scalar_prefetch=1,
            grid=(pairs,),
            in_specs=[
                pl.BlockSpec((1, tok, 128), lambda p, info: (0, 0, p)),
                col(pairs),
                col(2 * pairs),
            ],
            out_specs=[
                pl.BlockSpec((tok, 128), lambda p, info: (0, p)),
                pl.BlockSpec((tok, 128), lambda p, info: (0, p)),
                pl.BlockSpec((tok, 128), lambda p, info: (0, 0)),
                pl.BlockSpec((8, tok), lambda p, info: (0, 0)),
            ],
            scratch_shapes=[
                pltpu.VMEM((n // 2, tok, tok), F32),
                pltpu.VMEM((tok, 128), F32),
                pltpu.VMEM((tok, 128), F32),
                pltpu.VMEM((tok, 128), F32),
            ],
        ),
        out_shape=[
            jax.ShapeDtypeStruct((tok, heads * DH), F32),
            jax.ShapeDtypeStruct((tok, heads * DH), BF16),
            jax.ShapeDtypeStruct((tok, 128), F32),
            jax.ShapeDtypeStruct((8, tok), F32),
        ],
        compiler_params=params(18, n),
        cost_estimate=cost(11),
        name="attend",
    )(info, qkv, qkv, qkv)


def context_grad_kernel(gb, w, o, do_ref, delta_ref, drow_ref):
    do = dot_nn(gb[...], w[...]).astype(BF16)
    do_ref[...] = do
    prod = do.astype(F32) * o[...]
    lane = lax.broadcasted_iota(jnp.int32, (1, 128), 1)
    delta = jnp.zeros(delta_ref.shape, F32)
    for g in range(prod.shape[1] // 128):
        piece = prod[:, g * 128 : (g + 1) * 128]
        for j in range(2):
            in_head = (lane < 64) if j == 0 else (lane >= 64)
            value = jnp.sum(jnp.where(in_head, piece, 0.0), axis=1, keepdims=True)
            delta = jnp.where(lane == 2 * g + j, value, delta)
    delta_ref[...] = delta
    drow_ref[...] = delta.T[:8]


def context_grad(gb, w, o):
    tok, cols = o.shape
    return pl.pallas_call(
        context_grad_kernel,
        out_shape=[
            jax.ShapeDtypeStruct((tok, cols), BF16),
            jax.ShapeDtypeStruct((tok, 128), F32),
            jax.ShapeDtypeStruct((8, tok), F32),
        ],
        compiler_params=params(12),
        cost_estimate=cost(1.5),
        name="context_grad",
    )(gb, w, o)


def query_grad_kernel(n, info, q_ref, k_ref, v_ref, do_ref, lse_ref, delta_ref, dq_ref, dqt_ref, acc):
    p = pl.program_id(0)
    c, length, first = info[0], info[1], info[2]
    half = n // 2
    tok = q_ref.shape[1]
    my_block = c // half
    lane = lax.broadcasted_iota(jnp.int32, (1, 128), 1)
    row = lax.broadcasted_iota(jnp.int32, (tok, 1), 0) + c * tok
    q2 = q_ref[0] * jnp.asarray(DH**-0.5, BF16)
    do2 = do_ref[...]
    outs = []
    for j in range(2):
        pair = info[3 + 2 * p + j]
        in_head = (lane < 64) if j == 0 else (lane >= 64)
        qm = jnp.where(in_head, q2, jnp.zeros_like(q2))
        dom = jnp.where(in_head, do2, jnp.zeros_like(do2))
        some = jnp.logical_not((pair == 1) & (my_block == 0))
        block = my_block ^ pair
        pick = lane == 2 * p + j
        lse = jnp.sum(jnp.where(pick, lse_ref[...], 0.0), axis=1, keepdims=True)
        lse = jnp.where(row < length, lse, -LOW)
        delta = jnp.sum(jnp.where(pick, delta_ref[...], 0.0), axis=1, keepdims=True)
        acc[...] = jnp.zeros_like(acc)

        def chunk(i, _):
            kstart = (block * half + ((c % half) ^ i)) * tok
            reach = jnp.where(pair == 1, n * tok, jnp.maximum(first, (c + 1) * tok))
            needed = some & (kstart < jnp.minimum(length, reach))
            clear = jnp.where(pair == 1, n * tok, jnp.maximum(first, c * tok + 1))
            full = kstart + tok <= jnp.minimum(length, clear)

            def work(masked):
                k = k_ref[i + pair * half]
                s = dot_nt(qm, k)
                if masked:
                    kpos = kstart + lax.broadcasted_iota(jnp.int32, (1, tok), 1)
                    s = jnp.where(allowed_of(row, kpos, first, length), s, LOW)
                e = jnp.exp(s - lse)
                dp = dot_nt(dom, v_ref[i + pair * half])
                ds = (e * (dp - delta)).astype(BF16)
                acc[...] += dot_nn(ds, k)

            @pl.when(needed & full)
            def _():
                work(False)

            @pl.when(needed & jnp.logical_not(full))
            def _():
                work(True)

            return 0

        lax.fori_loop(0, half, chunk, 0)
        outs.append(acc[...])
    dq = jnp.where(lane < 64, outs[0], outs[1]) * DH**-0.5
    dq_ref[...] = dq.astype(BF16)
    dqt_ref[...] = dq.T.astype(BF16)


def query_grad(info, qkv, do, lse, delta, heads):
    n, tok, _ = qkv.shape
    pairs = heads // 2
    col = lambda at: pl.BlockSpec((n, tok, 128), lambda p, info: (0, 0, at + p))
    own = pl.BlockSpec((tok, 128), lambda p, info: (0, p))
    stat = pl.BlockSpec((tok, 128), lambda p, info: (0, 0))
    return pl.pallas_call(
        functools.partial(query_grad_kernel, n),
        grid_spec=pltpu.PrefetchScalarGridSpec(
            num_scalar_prefetch=1,
            grid=(pairs,),
            in_specs=[
                pl.BlockSpec((1, tok, 128), lambda p, info: (0, 0, p)),
                col(pairs),
                col(2 * pairs),
                own,
                stat,
                stat,
            ],
            out_specs=[own, pl.BlockSpec((128, tok), lambda p, info: (p, 0))],
            scratch_shapes=[pltpu.VMEM((tok, 128), F32)],
        ),
        out_shape=[
            jax.ShapeDtypeStruct((tok, heads * DH), BF16),
            jax.ShapeDtypeStruct((heads * DH, tok), BF16),
        ],
        compiler_params=params(12, n),
        cost_estimate=cost(10),
        name="query_grad",
    )(info, qkv, qkv, qkv, do, lse, delta)


def key_grad_kernel(n, info, q_ref, k_ref, v_ref, *refs):
    p = pl.program_id(0)
    c, length, first = info[0], info[1], info[2]
    half = n // 2
    do_refs, stat_refs = refs[:half], refs[half : 2 * half]
    dk_ref, dv_ref, dt_ref, do_scr, stat, kacc, vacc = refs[2 * half :]
    for i in range(half):
        do_scr[i] = do_refs[i][...]
        stat[i] = stat_refs[i][...]
    tok = k_ref.shape[1]
    my_block = c // half
    lane = lax.broadcasted_iota(jnp.int32, (1, 128), 1)
    kpos = lax.broadcasted_iota(jnp.int32, (tok, 1), 0) + c * tok
    kstart = c * tok
    k2 = k_ref[0] * jnp.asarray(DH**-0.5, BF16)
    v2 = v_ref[0]
    dks, dvs = [], []
    for j in range(2):
        h = 2 * p + j
        pair = info[3 + h]
        in_head = (lane < 64) if j == 0 else (lane >= 64)
        km = jnp.where(in_head, k2, jnp.zeros_like(k2))
        vm = jnp.where(in_head, v2, jnp.zeros_like(v2))
        some = jnp.logical_not((pair == 1) & (my_block == 1)) & (kstart < length)
        block = my_block ^ pair
        kacc[...] = jnp.zeros_like(kacc)
        vacc[...] = jnp.zeros_like(vacc)

        def chunk(i, _):
            at = block * half + ((c % half) ^ i)
            qstart = at * tok
            d = i + pair * half
            needed = some & (qstart < length) & ((pair == 1) | (at >= c) | (kstart < first))
            full = (pair == 1) | (at > c) | (kstart + tok <= first)

            def work(masked):
                q = q_ref[d]
                do = do_scr[i]
                qpos = qstart + lax.broadcasted_iota(jnp.int32, (1, tok), 1)
                lse = jnp.where(qpos < length, stat[i, pl.ds(h, 1), :], -LOW)
                s = dot_nt(km, q)
                if masked:
                    s = jnp.where((kpos < first) | (kpos <= qpos), s, LOW)
                e = jnp.exp(s - lse)
                vacc[...] += dot_nn(e.astype(BF16), do)
                dp = dot_nt(vm, do)
                ds = (e * (dp - stat[i, pl.ds(8 + h, 1), :])).astype(BF16)
                kacc[...] += dot_nn(ds, q)

            @pl.when(needed & full)
            def _():
                work(False)

            @pl.when(needed & jnp.logical_not(full))
            def _():
                work(True)

            return 0

        lax.fori_loop(0, half, chunk, 0)
        good = kpos < length
        dks.append(jnp.where(good, kacc[...], 0.0))
        dvs.append(jnp.where(good, vacc[...], 0.0))
    dk = jnp.where(lane < 64, dks[0], dks[1]) * DH**-0.5
    dv = jnp.where(lane < 64, dvs[0], dvs[1])
    dk_ref[...] = dk.astype(BF16)
    dv_ref[...] = dv.astype(BF16)
    dt_ref[0] = dk.T.astype(BF16)
    dt_ref[1] = dv.T.astype(BF16)


def key_grad(info, qkv, do_parts, stat_parts, heads):
    n, tok, _ = qkv.shape
    pairs = heads // 2
    half = n // 2
    own = lambda at: pl.BlockSpec((1, tok, 128), lambda p, info: (0, 0, at + p))
    every = pl.BlockSpec((n, tok, 128), lambda p, info: (0, 0, p))
    stat = pl.BlockSpec((16, tok), lambda p, info: (0, 0))
    out = pl.BlockSpec((tok, 128), lambda p, info: (0, p))
    return pl.pallas_call(
        functools.partial(key_grad_kernel, n),
        grid_spec=pltpu.PrefetchScalarGridSpec(
            num_scalar_prefetch=1,
            grid=(pairs,),
            in_specs=[every, own(pairs), own(2 * pairs)] + [out] * half + [stat] * half,
            out_specs=[out, out, pl.BlockSpec((2, 128, tok), lambda p, info: (0, p, 0))],
            scratch_shapes=[
                pltpu.VMEM((half, tok, 128), BF16),
                pltpu.VMEM((half, 16, tok), F32),
                pltpu.VMEM((tok, 128), F32),
                pltpu.VMEM((tok, 128), F32),
            ],
        ),
        out_shape=[jax.ShapeDtypeStruct((tok, heads * DH), BF16)] * 2
        + [jax.ShapeDtypeStruct((2, heads * DH, tok), BF16)],
        compiler_params=params(14, n),
        cost_estimate=cost(11),
        name="key_grad",
    )(info, qkv, qkv, qkv, *do_parts, *stat_parts)


def token_grad_kernel(dq, dk, dv, w, out):
    out[...] = (dot_nt(dq[...], w[0]) + dot_nt(dk[...], w[1]) + dot_nt(dv[...], w[2])).astype(BF16)


def token_grad(dq, dk, dv, w):
    return pl.pallas_call(
        token_grad_kernel,
        out_shape=jax.ShapeDtypeStruct((dq.shape[0], w.shape[1]), BF16),
        compiler_params=params(12),
        cost_estimate=cost(2.5),
        name="token_grad",
    )(dq, dk, dv, w)


def place_kernel(split, info, mine, other, *outs):
    c = info[0]
    g = pl.program_id(0)
    for i, out in enumerate(outs):
        if len(outs) == 1:
            place_rows(c, mine, other, out)
        else:
            pl.when((g < split) if i == 0 else (g >= split))(functools.partial(place_rows, c, mine, other, out))


def place_rows(c, mine, other, out):
    x = c % 2
    rows = mine.shape[0] // 4
    for i in range(4):
        z = (c // 2) ^ i
        for side, ref in ((x, mine), (1 - x, other)):
            at = pl.multiple_of((side * 4 + z) * rows, 8)
            out[pl.ds(at, rows), :] = ref[i * rows : (i + 1) * rows, :].astype(F32)


def place(info, mine, other, widths):
    rows, cols = mine.shape
    wide = 384
    split = widths[0] // wide
    maps = [
        lambda g, info: (0, jnp.minimum(g, split - 1)),
        lambda g, info: (0, jnp.maximum(g - split, 0)),
    ]
    return pl.pallas_call(
        functools.partial(place_kernel, split),
        grid_spec=pltpu.PrefetchScalarGridSpec(
            num_scalar_prefetch=1,
            grid=(cols // wide,),
            in_specs=[pl.BlockSpec((rows, wide), lambda g, info: (0, g))] * 2,
            out_specs=[pl.BlockSpec((2 * rows, wide), maps[i]) for i in range(len(widths))],
        ),
        out_shape=[jax.ShapeDtypeStruct((2 * rows, w), F32) for w in widths],
        compiler_params=params(16),
        cost_estimate=cost(3),
        name="place",
    )(info, mine, other)


def sequence_product_kernel(n, spot, q_ref, kv_ref, own, *refs):
    halves = refs[: 2 * n - 2]
    keep, send = refs[2 * n - 2 :]
    c, s, t = spot[0], spot[1], spot[2]
    few, many = q_ref.shape[1], kv_ref.shape[1]
    rows = few + many
    tok = q_ref.shape[2]
    total = None
    added = jnp.zeros((rows, 128), F32)
    for d in range(n):
        at = c ^ d
        for e in range(2):
            if d == 0:
                where = e * (tok // 2)
                right = own[e * (tok // 2) : (e + 1) * (tok // 2), :]
            else:
                where = pl.multiple_of((t if e == 0 else 1 - t) * (tok // 2), tok // 2)
                right = halves[2 * (d - 1) + e][...]
            span = pl.ds(where, tok // 2)
            left = jnp.concatenate([q_ref[at, :, span], kv_ref[at, :, span]], axis=0)
            value = dot_nn(left, right)
            total = value if total is None else total + value
            added += lane_groups(jnp.add, left.astype(F32))
    sums = jnp.sum(added, axis=1, keepdims=True)
    high = sums.astype(BF16).astype(F32)
    lane = lax.broadcasted_iota(jnp.int32, (1, 128), 1)
    split = jnp.where(lane == 0, high, jnp.where(lane == 1, sums - high, 0.0))
    line = jnp.concatenate([split, jnp.zeros((256 - rows, 128), F32)], axis=0).T[:16]
    cols = keep.shape[1]
    line = jnp.concatenate([line, jnp.zeros((16, cols - 256), F32)], axis=1)
    if total.shape[1] == 2 * cols:
        first = s == 0
        keep[:rows, :] = jnp.where(first, total[:, :cols], total[:, cols:])
        send[:rows, :] = jnp.where(first, total[:, cols:], total[:, :cols]).astype(BF16)
    else:
        keep[:rows, :] = total
        send[:rows, :] = total.astype(BF16)
    keep[rows:, :] = line
    send[rows:, :] = line.astype(BF16)


def sequence_product(spot, q_parts, kv_parts, own, halves, cols):
    n, few, tok = q_parts.shape
    rows = few + kv_parts.shape[1]
    width = own.shape[1]
    every = [half for pair in halves for half in pair]
    whole = lambda shape: pl.BlockSpec(shape, lambda i, info: (0,) * len(shape))
    out = whole((rows + 16, cols))
    return pl.pallas_call(
        functools.partial(sequence_product_kernel, n),
        grid_spec=pltpu.PrefetchScalarGridSpec(
            num_scalar_prefetch=1,
            grid=(1,),
            in_specs=[whole(q_parts.shape), whole(kv_parts.shape), whole((tok, width))]
            + [whole((tok // 2, width))] * len(every),
            out_specs=[out, out],
        ),
        out_shape=[
            jax.ShapeDtypeStruct((rows + 16, cols), F32),
            jax.ShapeDtypeStruct((rows + 16, cols), BF16),
        ],
        compiler_params=params(24),
        cost_estimate=cost(6),
        name="sequence_product",
    )(spot, q_parts, kv_parts, own, *every)


def place_turned_kernel(n, part, out, line, scr):
    rows = part.shape[1] - 16
    small = rows // 3
    hdl = n * small
    for at in range(n):
        block = part[at].astype(F32)
        scr[at * small : (at + 1) * small, :] = block[:small]
        scr[hdl + at * 2 * small : hdl + (at + 1) * 2 * small, :] = block[small:rows]
        line[at] = block[rows : rows + 8]
    for m in range(3):
        out[m] = scr[m * hdl : (m + 1) * hdl, :].T


def place_turned(parts):
    n, rows, cols = parts.shape
    wide = n * (rows - 16)
    return pl.pallas_call(
        functools.partial(place_turned_kernel, n),
        out_shape=[
            jax.ShapeDtypeStruct((3, cols, wide // 3), F32),
            jax.ShapeDtypeStruct((n, 8, cols), F32),
        ],
        scratch_shapes=[pltpu.VMEM((wide, cols), F32)],
        compiler_params=params(16),
        cost_estimate=cost(2),
        name="place_turned",
    )(parts)


def spread(x):
    n = lax.axis_size("ctx")
    return lax.all_to_all(jnp.broadcast_to(x[None], (n,) + x.shape), "ctx", 0, 0)


def outer(a, b):
    return lax.dot_general(a, b, (((0,), (0,)), ((), ())), preferred_element_type=F32)


def shard_columns(x, other):
    s = lax.axis_index("shard")
    cols = x.shape[1] // 2
    return lax.dynamic_slice_in_dim(x, (1 - s if other else s) * cols, cols, 1)


def fast_mesh():
    return lax.axis_size("shard") == 2 and lax.axis_size("ctx") == 8


def own_rows(grads):
    grad = jnp.concatenate(grads, axis=1).astype(BF16)
    return lax.psum_scatter(grad, "shard", scatter_dimension=0, tiled=True)


def add_rounded(kept, got):
    return (kept.astype(F32) + got.astype(F32)).astype(BF16)


def cut_by_x(x):
    half = x.shape[0] // 2
    at = lax.axis_index("ctx") % 2
    keep = lax.dynamic_slice_in_dim(x, at * half, half, 0)
    return keep, lax.dynamic_slice_in_dim(x, (1 - at) * half, half, 0)


def along_z(x):
    rows, cols = x.shape
    lines = [[0, 2, 4, 6], [1, 3, 5, 7]]
    return lax.all_to_all(x.reshape(4, rows // 4, cols), "ctx", 0, 0, axis_index_groups=lines)


def add_up(pieces):
    return jnp.sum(pieces.astype(F32), axis=0).astype(BF16)


def body(
    tokens, teacher, w_qkv, b_qv, w_out, w_up, b_up, w_down, biases, gains, lengths, prefix, pairing
):
    tok, width = tokens.shape
    n_shard = lax.axis_size("shard")
    n = lax.axis_size("ctx")
    c = lax.axis_index("ctx").astype(jnp.int32)
    t = lax.axis_index("tp").astype(jnp.int32)
    length = lengths[0]
    heads = pairing.shape[1]
    hdl = heads * DH
    info = jnp.concatenate([c[None], lengths, prefix, pairing[0]])
    core = t[None]
    zero = jnp.zeros((1,), jnp.int32)

    full_qkv = gather_rows(w_qkv.transpose(1, 0, 2))
    token_parts = gather_ctx_halves(tokens)
    near = token_parts[2][0]
    full_out = gather_rows(after(w_out, near)[None])[0]
    full_up = gather_rows(after(w_up, near)[None])[0]
    full_down = gather_rows(after(w_down, near)[None])[0]
    ffl = full_up.shape[1]
    bias_qkv = jnp.concatenate([b_qv[0], jnp.zeros((hdl,), F32), b_qv[1]])[None]

    half = tok // 2
    own_halves = [(tokens[:half], tokens[half:])]
    qkv = project_into(None, n, range(0, 1, 1), zero, own_halves, full_qkv, bias_qkv)
    for blocks in (range(2, n, 2), range(1, n, 2)):
        halves = [token_parts[d] for d in blocks]
        qkv = project_into(qkv, n, blocks, core, halves, full_qkv, bias_qkv)
    context, o_r, lse, lse_row = attend(info, qkv, heads)
    branch = tp_sum(dot_nt(o_r, full_out).astype(BF16)) + biases[0]

    xf = tokens.astype(F32)
    hidden, pull_first = jax.vjp(normalize, xf + branch, gains[0], biases[2])
    hidden_r = hidden.astype(BF16)
    upper = jnp.dot(hidden_r, full_up, preferred_element_type=F32) + b_up
    active, pull_gelu = jax.vjp(gelu_exact, upper)
    active_r = active.astype(BF16)
    feed = tp_sum(dot_nt(active_r, full_down).astype(BF16)) + biases[1]
    output, pull_second = jax.vjp(normalize, hidden + feed, gains[1], biases[3])
    qpos = c * tok + jnp.arange(tok, dtype=jnp.int32)
    valid = (qpos < length)[:, None]
    error = jnp.where(valid, output - teacher.astype(F32), 0.0)
    d_second, d_gain2, d_shift2 = pull_second(error)
    d_feed = d_second.astype(BF16)
    d_active = jnp.dot(d_feed, full_down, preferred_element_type=F32)
    d_upper = pull_gelu(d_active)[0].astype(BF16)
    d_hidden = d_second + tp_sum(dot_nt(d_upper, full_up).astype(BF16))
    d_first, d_gain1, d_shift1 = pull_first(d_hidden)
    d_branch = d_first.astype(BF16)

    d_context, delta, delta_row = context_grad(d_branch, full_out, context)
    swapped = pairing[0] == 1
    do_parts = gather_block(d_context, jnp.repeat(swapped, DH)[None])
    stats = jnp.concatenate([lse_row, delta_row], axis=0)
    swapped8 = jnp.concatenate([swapped, jnp.zeros((8 - heads,), bool)])
    stat_parts = gather_block(stats, jnp.concatenate([swapped8, swapped8])[:, None])
    dq_r, dq_t = query_grad(info, qkv, d_context, lse, delta, heads)
    down, rest = [(d_feed, active_r)], [(hidden_r, d_upper), (d_branch, o_r)]
    side = lambda parts: parts[0] if len(parts) == 1 else jnp.concatenate(parts, axis=1)
    if fast_mesh():
        part = []
        for pairs in (down, rest):
            sent = [flip(outer(shard_columns(x, True), y).astype(BF16), "shard", 1) for x, y in pairs]
            kept = [outer(shard_columns(x, False), y) for x, y in pairs]
            part.append(side([add_rounded(k, g) for k, g in zip(kept, sent)]))
        keep_down, send_down = cut_by_x(part[0])
        half_down = add_rounded(keep_down, flip(send_down, "ctx", 1))
        keep_rest, send_rest = cut_by_x(part[1])
        half_rest = add_rounded(keep_rest, flip(after(send_rest, *do_parts), "ctx", 1))
        line_down = along_z(after(half_down, *do_parts))

    err_sum = jnp.sum(error * error)
    count = jnp.sum(valid.astype(F32))
    split = lambda rows: rows.reshape(rows.shape[0], n_shard, -1).transpose(1, 0, 2).reshape(n_shard, -1)
    early = jnp.concatenate(
        [
            split(jnp.sum(d_branch.astype(F32), axis=0)[None]),
            split(jnp.sum(d_feed.astype(F32), axis=0)[None]),
            split(d_shift1[None]),
            split(d_shift2[None]),
            split(d_gain1[None]),
            split(d_gain2[None]),
            split(jnp.sum(d_upper.astype(F32), axis=0)[None]),
            jnp.full((n_shard, 1), err_sum),
            jnp.full((n_shard, 1), count),
        ],
        axis=1,
    )
    early = ctx_sum(shard_scatter(early))[0]

    info_k = after(info, early)
    dk_r, dv_r, dkv_t = key_grad(info_k, qkv, do_parts, stat_parts, heads)
    moved_q = lax.all_to_all(after(dq_t, *do_parts).reshape(n, hdl // n, tok), "ctx", 0, 0)
    moved_kv = lax.all_to_all(dkv_t.reshape(n, 2 * hdl // n, tok), "ctx", 0, 0)
    grad_tokens = d_first + tp_sum(token_grad(dq_r, dk_r, dv_r, full_qkv))

    spot = jnp.stack([c, lax.axis_index("shard").astype(jnp.int32), t])
    cols = width // 2 if n_shard == 2 else width
    halves = [token_parts[d] for d in range(1, n)]
    keep, send = sequence_product(spot, moved_q, moved_kv, tokens, halves, cols)
    if n_shard == 2:
        total = (keep + flip(send, "shard", 1).astype(F32)).astype(BF16)
        grad_w_qkv, lines = place_turned(spread(total))
    else:
        rows = send.shape[0] - 16
        total = lax.psum_scatter(send[:rows], "shard", scatter_dimension=1, tiled=True)
        every = lax.all_gather(total, "ctx", axis=0, tiled=False)
        small = rows // 3
        every = jnp.concatenate(
            [every[:, :small].reshape(n * small, -1), every[:, small:].reshape(2 * n * small, -1)]
        )
        grad_w_qkv = every.reshape(3, hdl, -1).transpose(0, 2, 1).astype(F32)
        line = lax.psum(keep[rows : rows + 8], "shard")
        lines = lax.all_gather(line, "ctx", axis=0, tiled=False)
    bias_sums = lines[:, 0] + lines[:, 1]
    small = hdl // n
    sums_q = bias_sums[:, :small].reshape(hdl)
    sums_v = bias_sums[n // 2 :, small : 3 * small].reshape(hdl)
    grad_b_qv = jnp.stack([sums_q, sums_v])
    mine = hdl // n_shard
    grad_b_qv = lax.dynamic_slice_in_dim(grad_b_qv, lax.axis_index("shard") * mine, mine, 1)
    if fast_mesh():
        sum_down = add_up(line_down)
        line_rest = along_z(half_rest)
        every_down = [sum_down] + [flip(sum_down, "ctx", d) for d in (2, 4, 6)]
        sum_rest = add_up(after(line_rest, send))
        every_rest = [sum_rest] + [flip(sum_rest, "ctx", d) for d in (2, 4, 6)]
        every_down = jnp.concatenate(every_down, axis=0)
        (grad_w_down,) = place(info, every_down, flip(after(every_down, send), "ctx", 1), (ffl,))
        every_rest = jnp.concatenate(every_rest, axis=0)
        grad_w_up, grad_w_out = place(
            info, every_rest, flip(after(every_rest, total), "ctx", 1), (ffl, hdl)
        )
    else:
        sums = [
            lax.psum(own_rows([outer(x, y) for x, y in pairs]), "ctx").astype(F32)
            for pairs in (down, rest)
        ]
        grad_w_down = sums[0]
        grad_w_up, grad_w_out = sums[1][:, :ffl], sums[1][:, ffl:]

    wide = width // n_shard
    grad_biases = early[: 4 * wide].reshape(4, wide)
    grad_gains = early[4 * wide : 6 * wide].reshape(2, wide)
    grad_b_up = early[6 * wide : 6 * wide + ffl // n_shard]
    loss = early[-2] / (early[-1] * width)
    return (
        output,
        loss,
        grad_tokens,
        grad_w_qkv.transpose(1, 0, 2),
        grad_w_out,
        grad_w_up,
        grad_w_down,
        grad_b_qv,
        grad_b_up,
        grad_biases,
        grad_gains,
    )


def solution(mesh):
    return jax.shard_map(
        body,
        mesh=mesh,
        in_specs=(
            P(("shard", "ctx"), None),
            P(("shard", "ctx"), None),
            P("shard", None, "tp"),
            P(None, "tp"),
            P("shard", "tp"),
            P("shard", "tp"),
            P("tp"),
            P("shard", "tp"),
            P(),
            P(),
            P("shard"),
            P("shard"),
            P("shard", "tp"),
        ),
        out_specs=(
            P(("shard", "ctx"), None),
            P(),
            P(("shard", "ctx"), None),
            P("shard", None, "tp"),
            P("shard", "tp"),
            P("shard", "tp"),
            P("shard", "tp"),
            P(None, ("tp", "shard")),
            P(("tp", "shard")),
            P(None, "shard"),
            P(None, "shard"),
        ),
        check_vma=False,
    )
```
